32 devices in a mesh: dp: 8 (over y, x, core), tensor: 4 (over z).
Axes of the slice: x: 2, y: 2, z: 4, core: 2. Of those that a mesh axis runs over, the one named last changes fastest.
Arguments:
- block_input: bfloat16 [4096, 768], P('dp'), may hold values from -6 to 6
- attn_gain: bfloat16 [768], P('dp'), may hold values from 0.25 to 1.75
- query_weight: bfloat16 [768, 768], P('dp', 'tensor'), may hold values from -0.21875 to 0.21875
- key_weight: bfloat16 [768, 768], P('dp', 'tensor'), may hold values from -0.21875 to 0.21875
- value_weight: bfloat16 [768, 768], P('dp', 'tensor'), may hold values from -0.21875 to 0.21875
- output_weight: bfloat16 [768, 768], P('dp', 'tensor'), may hold values from -0.875 to 0.875
- bias_table: float32 [12, 32], P('tensor'), may hold values from -6 to 306
- ffn_gain: bfloat16 [768], P('dp'), may hold values from 0.25 to 1.75
- router_weight: bfloat16 [768, 8], P('dp'), may hold values from -0.4375 to 0.4375
- expert_in: bfloat16 [8, 768, 3072], P('dp', None, 'tensor'), may hold values from -0.21875 to 0.21875
- expert_out: bfloat16 [8, 3072, 768], P('dp', 'tensor'), may hold values from -0.21875 to 0.21875
- expert_ids: int32 [4096, 2], P('dp'), may hold values from 0 to 7, all different within a row; in each aligned block of 512 rows (0 to 511, 512 to 1023, ...) at most 152 rows name the same one
- out_cotangent: bfloat16 [4096, 768], P('dp'), may hold values from -6 to 6
Outputs:
- block_output: bfloat16 [4096, 768], P('dp', 'tensor')
- input_grad: float32 [4096, 768], P('dp', 'tensor')
- attn_gain_grad: float32 [768], P('dp')
- query_grad: float32 [768, 768], P('dp', 'tensor')
- key_grad: float32 [768, 768], P('dp', 'tensor')
- value_grad: float32 [768, 768], P('dp', 'tensor')
- output_grad: float32 [768, 768], P('dp', 'tensor')
- bias_grad: float32 [12, 32], P('tensor')
- ffn_gain_grad: float32 [768], P('dp')
- router_grad: float32 [768, 8], P('dp')
- expert_in_grad: float32 [8, 768, 3072], P('dp', None, 'tensor')
- expert_out_grad: float32 [8, 3072, 768], P('dp', 'tensor')
The draws below stay inside these ranges and needn't reach their ends.
Inputs may be any that keep to these rules, and one draw needn't show every extreme that they name: `expert_ids`: the two experts of a token differ; among the tokens of one dp index no expert is named more than 152 times.
All inputs are finite; a program needn't handle non-finite values.
Results may differ from the reference program's by a relative error of at most 0.018.
Values may be sent and summed in bfloat16 or wider, within the bound.
A program may use at most 320 MiB of HBM per device.

```python
import math
import jax
import jax.numpy as jnp
import numpy as np
from jax import lax

D = 768
HEADS = 12
HEAD_DIM = 64
FF = 3072
NB = 32
SEQ_LEN = 512
HD_ALL = 768
EXPERTS = 8
TOK_DEV = 512
TOKENS = 4096
CAP = 152
N_DP = 8


def draw_bias_table(key, part):
    baseline_key = jax.random.fold_in(key, 0)
    baseline = 1.5 * jax.random.truncated_normal(baseline_key, -4.0, 4.0, (HEADS, NB), jnp.float32)
    return baseline


def with_spikes(array, key, source, target, parts, factor):
    def block_of(position):
        return (jnp.arange(array.shape[position]) // (array.shape[position] // parts)).reshape((-1,) + (1,) * (array.ndim - 1 - position))

    one_side = jax.random.permutation(key, parts)[block_of(target)]
    second = (block_of(target) + parts // 2) % parts
    return jnp.where((block_of(source) == one_side) | (block_of(source) == second), factor * array, array)


def block_scale(stream_key, extent, cuts, least, high):
    loudness, own = 1.0, jax.random.fold_in(stream_key, 6)
    for dim, blocks in cuts:
        heights = jnp.exp(jax.random.uniform(jax.random.fold_in(own, dim), (blocks,), jnp.float32, least / len(cuts), high / len(cuts)))
        loudness = loudness * jnp.repeat(heights, extent[dim] // blocks).reshape([-1 if axis == dim else 1 for axis in range(len(extent))])
    return loudness


def shared_out(rng, own, number, rows, number_of, top, reach, lean):
    sequence = jax.random.permutation(rng, number_of)
    heavy_load, ordinary = load_shares(number_of, rows * top, reach, lean, True), load_shares(number_of, rows * top, reach, lean, False)
    places = jnp.arange(number_of)

    def named(lengths, offset_by):
        used = int((lengths > 0).sum())
        fixed = max(1, used // 4)
        passed = fixed + (places - fixed + offset_by * (used - fixed)) % max(1, number_of - fixed)
        return jnp.zeros((number_of,), jnp.int32).at[sequence[jnp.where(places < fixed, places, passed)]].set(jnp.asarray(lengths, jnp.int32))

    lengths = jnp.where(number % 4 == 0, named(heavy_load, number // 4), named(ordinary, number - number // 4 - 1))
    mixed = jax.random.permutation(jax.random.fold_in(own, 3), number_of)
    donor, taker = mixed[0:number_of // 2 * 2:2], mixed[1:number_of // 2 * 2:2]
    slack = jnp.minimum(lengths[donor] - 1, reach - lengths[taker]) // 2
    slack = jnp.where((donor == sequence[0]) | (taker == sequence[0]) | (lengths[taker] == 0), 0, jnp.maximum(slack, 0))
    passed = jax.random.randint(jax.random.fold_in(own, 4), (number_of // 2,), 0, 1 << 20) % (slack + 1)
    lengths = lengths.at[donor].add(-passed).at[taker].add(passed)
    items = jnp.searchsorted(jnp.cumsum(lengths), jnp.arange(rows * top), side="right").astype(jnp.int32)
    table = items.reshape(top, rows).T
    table = table[jax.random.permutation(jax.random.fold_in(own, 1), rows)]
    offset_by = jax.random.randint(jax.random.fold_in(own, 2), (rows, 1), 0, top)
    return jnp.take_along_axis(table, (jnp.arange(top)[None, :] + offset_by) % top, axis=1)


def load_shares(count, total, most, skew, full):
    loads = [(1 << 20) // math.isqrt(grade ** skew) + 1 for grade in range(1, count + 1)]
    largest = most if full else min(most, max(-(-total // count), total * loads[0] // sum(loads)))
    least = 1 if total - largest >= count - 1 else 0
    counts, spare = [largest] + [least] * (count - 1), total - largest - least * (count - 1)
    while spare > 0:
        candidates = [i for i in range(1, count) if counts[i] < largest] or [i for i in range(1, count) if counts[i] < most]
        pool, budget = sum([loads[i] for i in candidates]), spare
        for i in candidates:
            extra = min(most - counts[i], max(1, budget * loads[i] // pool), spare)
            counts[i] = counts[i] + extra
            spare = spare - extra
    return np.array(counts)


def noise(rng, dims, deviation, most, pieces=(), held_as=jnp.bfloat16):
    factor_of = block_scale(rng, dims, pieces, -0.22, 0.18) if pieces else 1.0
    values = jax.random.normal(rng, dims, jnp.float32) * deviation * factor_of
    return jnp.minimum(jnp.maximum(values, -most), most).astype(held_as)


def noise_with(key, extent, deviation, bound, cuts, heavy, held_as=jnp.bfloat16):
    array = deviation * jax.random.normal(key, extent, jnp.float32)
    if cuts:
        array = array * block_scale(key, extent, cuts, -0.22, 0.18)
    return jnp.clip(with_spikes(array, jax.random.fold_in(key, 3), *heavy), -bound, bound).astype(held_as)


def setup_inputs(seed: int = 0) -> dict:
    arg_keys = jax.random.split(jax.random.key(seed), 14)
    block_input = noise_with(arg_keys[0], (TOKENS, D), 1.0, 6.0, ((0, 8),), (0, 1, 8, 2.0))
    attn_gain = jnp.clip(1.0 + 0.15 * jax.random.normal(arg_keys[1], (D,), jnp.float32), 0.25, 1.75).astype(jnp.bfloat16)
    query_weight = noise(arg_keys[2], (D, HD_ALL), D ** -0.5, 0.21875, ((0, 8), (1, 4)))
    key_weight = noise(arg_keys[3], (D, HD_ALL), D ** -0.5, 0.21875, ((0, 8), (1, 4)))
    value_weight = noise(arg_keys[4], (D, HD_ALL), D ** -0.5, 0.21875, ((0, 8), (1, 4)))
    output_weight = noise(arg_keys[5], (D, HD_ALL), (HD_ALL // 16) ** -0.5, 0.875, ((0, 8), (1, 4)))
    bias_table = draw_bias_table(jax.random.fold_in(arg_keys[13], 71), 0)
    ffn_gain = jnp.clip(1.0 + 0.15 * jax.random.normal(arg_keys[7], (D,), jnp.float32), 0.25, 1.75).astype(jnp.bfloat16)
    router_weight = noise(arg_keys[8], (D, EXPERTS), (D // 4) ** -0.5, 0.4375, ((0, 8),))
    expert_in = noise(arg_keys[9], (EXPERTS, D, FF), D ** -0.5, 0.21875, ((0, 8), (2, 4)))
    expert_out = noise(arg_keys[10], (EXPERTS, FF, D), (FF // 4) ** -0.5, 0.21875, ((0, 8), (1, 4)))
    expert_ids_keys = jax.random.split(jax.random.fold_in(arg_keys[11], 1), TOKENS // TOK_DEV)
    expert_ids_turns = jax.random.permutation(jax.random.fold_in(arg_keys[11], 3), TOKENS // TOK_DEV)
    expert_ids = jax.vmap(lambda own, number: shared_out(jax.random.fold_in(arg_keys[11], 2), own, number, TOK_DEV, EXPERTS, 2, CAP, 2))(expert_ids_keys, expert_ids_turns).reshape((TOKENS, 2))
    out_cotangent = noise_with(arg_keys[12], (TOKENS, D), 1.0, 6.0, ((0, 8),), (0, 1, 8, 2.0))
    return dict(block_input=block_input, attn_gain=attn_gain, query_weight=query_weight, key_weight=key_weight, value_weight=value_weight, output_weight=output_weight, bias_table=bias_table, ffn_gain=ffn_gain, router_weight=router_weight, expert_in=expert_in, expert_out=expert_out, expert_ids=expert_ids, out_cotangent=out_cotangent)


EPSILON = 1e-06
MASKED = -1e+30

def bucket_matrix(length, bucket_count):
    exact_count = bucket_count // 2
    steps_ids = jnp.arange(length, dtype=jnp.int32)
    distant = jnp.full((length,), exact_count, jnp.int32)
    for level_index in range(1, bucket_count - exact_count):
        border = int(math.ceil(exact_count * 8.0 ** (level_index / (bucket_count - exact_count))))
        distant = distant + (steps_ids >= border).astype(jnp.int32)
    bucket_vec = jnp.where(steps_ids < exact_count, steps_ids, distant).astype(jnp.int32)
    row_ids = lax.broadcasted_iota(jnp.int32, (length, length), 0)
    col_ids = lax.broadcasted_iota(jnp.int32, (length, length), 1)
    distance = jnp.maximum(row_ids - col_ids, 0).astype(jnp.int32)
    return (bucket_vec, distance, row_ids >= col_ids)

def rms_scale(matrix):
    return lax.rsqrt(lax.optimization_barrier(jnp.mean(matrix * matrix, axis=-1, keepdims=True)) + EPSILON)

def norm_back(dnormed, row_values, row_scale, gain_row):
    inner_mean = lax.optimization_barrier(jnp.mean(gain_row * dnormed * row_values, axis=-1, keepdims=True))
    return row_scale * (gain_row * dnormed - row_values * row_scale * row_scale * inner_mean)

def bucket_sums(grads, bucket_vec, bucket_count):
    head_count = grads.shape[0]
    length = grads.shape[1]
    flipped = grads[:, :, ::-1]
    padded = jnp.pad(flipped, ((0, 0), (0, 0), (0, length)))
    skewed = padded.reshape(head_count, 2 * length * length)[:, :length * (2 * length - 1)]
    skewed = skewed.reshape(head_count, length, 2 * length - 1)
    diagonal = lax.optimization_barrier(jnp.sum(skewed, axis=1))[:, length - 1:]
    labels = jnp.arange(bucket_count, dtype=jnp.int32)
    onehot = (bucket_vec[:, None] == labels[None, :]).astype(jnp.float32)
    return jnp.dot(diagonal, onehot, precision=lax.Precision.HIGHEST, preferred_element_type=jnp.float32)

def attention_scores(queries, key_rows, bias_heads, causal):
    factor = queries.shape[-1] ** (-0.5)
    products = jnp.einsum('qhd,khd->hqk', queries.astype(jnp.float32), key_rows.astype(jnp.float32))
    return jnp.where(causal[None], products * factor + bias_heads, MASKED)

def attend_forward(queries, key_rows, value_rows, bias_heads, causal):
    scores = attention_scores(queries, key_rows, bias_heads, causal)
    row_max = lax.optimization_barrier(jnp.max(scores, axis=-1, keepdims=True))
    row_total = lax.optimization_barrier(jnp.sum(jnp.exp(scores - row_max), axis=-1, keepdims=True))
    log_total = row_max + jnp.log(row_total)
    weights_low = jnp.exp(scores - log_total).astype(jnp.bfloat16)
    context = jnp.einsum('hqk,khd->qhd', weights_low.astype(jnp.float32), value_rows.astype(jnp.float32))
    return (context.astype(jnp.bfloat16), log_total)

def attend_backward(queries, key_rows, value_rows, bias_heads, causal, log_total, dcontext, bucket_vec, bucket_count):
    factor = queries.shape[-1] ** (-0.5)
    scores = attention_scores(queries, key_rows, bias_heads, causal)
    weights = jnp.exp(scores - log_total)
    weights_low = weights.astype(jnp.bfloat16)
    dweights = jnp.einsum('qhd,khd->hqk', dcontext.astype(jnp.float32), value_rows.astype(jnp.float32))
    dvalues = jnp.einsum('hqk,qhd->khd', weights_low.astype(jnp.float32), dcontext.astype(jnp.float32))
    agreement = lax.optimization_barrier(jnp.sum(weights * dweights, axis=-1, keepdims=True))
    dscores = weights * (dweights - agreement)
    dbias = bucket_sums(dscores, bucket_vec, bucket_count)
    dscores_low = dscores.astype(jnp.bfloat16).astype(jnp.float32)
    dqueries = factor * jnp.einsum('hqk,khd->qhd', dscores_low, key_rows.astype(jnp.float32))
    dkeys = factor * jnp.einsum('hqk,qhd->khd', dscores_low, queries.astype(jnp.float32))
    return (dqueries.astype(jnp.bfloat16), dkeys.astype(jnp.bfloat16), dvalues.astype(jnp.bfloat16), dbias)

def expert_forward(rows_in, weight_in, weight_out):
    pre_act = jnp.dot(rows_in, weight_in, preferred_element_type=jnp.float32)
    active = jax.nn.gelu(pre_act).astype(jnp.bfloat16)
    return (pre_act, active, jnp.dot(active, weight_out, preferred_element_type=jnp.float32))

def expert_backward(rows_in, pre_act, active, drows_in, weight_in, weight_out):
    dactive = jnp.dot(drows_in, weight_out.T, preferred_element_type=jnp.float32)
    unused_value, pullback = jax.vjp(jax.nn.gelu, pre_act)
    dpre_low = pullback(dactive)[0].astype(jnp.bfloat16)
    grad_out = jnp.dot(active.T, drows_in, preferred_element_type=jnp.float32)
    grad_in = jnp.dot(rows_in.T, dpre_low, preferred_element_type=jnp.float32)
    owner_back = jnp.dot(dpre_low, weight_in.T, preferred_element_type=jnp.float32)
    return (grad_in, grad_out, owner_back)

def reference(block_input, attn_gain, query_weight, key_weight, value_weight, output_weight, bias_table, ffn_gain, router_weight, expert_in, expert_out, expert_ids, out_cotangent):
    inputs_f = block_input.astype(jnp.float32)
    scale_one = rms_scale(inputs_f)
    gain_one = attn_gain.astype(jnp.float32)
    normed_one = (inputs_f * scale_one * gain_one).astype(jnp.bfloat16)
    queries = jnp.dot(normed_one, query_weight, preferred_element_type=jnp.float32).astype(jnp.bfloat16)
    key_rows = jnp.dot(normed_one, key_weight, preferred_element_type=jnp.float32).astype(jnp.bfloat16)
    value_rows = jnp.dot(normed_one, value_weight, preferred_element_type=jnp.float32).astype(jnp.bfloat16)
    bucket_vec, distance, causal = bucket_matrix(SEQ_LEN, NB)
    bias_heads = jnp.take(jnp.take(bias_table, bucket_vec, axis=1), distance, axis=1)
    seq_count = TOKENS // SEQ_LEN

    def split_heads(matrix):
        return matrix.reshape(seq_count, SEQ_LEN, HEADS, HEAD_DIM)

    def forward_one(triple):
        return attend_forward(triple[0], triple[1], triple[2], bias_heads, causal)
    context, log_total = lax.map(forward_one, (split_heads(queries), split_heads(key_rows), split_heads(value_rows)))
    context_flat = context.reshape(TOKENS, HD_ALL)
    attn_out = jnp.dot(context_flat, output_weight.T, preferred_element_type=jnp.float32)
    residual = inputs_f + attn_out
    scale_two = rms_scale(residual)
    gain_two = ffn_gain.astype(jnp.float32)
    normed_two = (residual * scale_two * gain_two).astype(jnp.bfloat16)
    logits = jnp.dot(normed_two, router_weight, preferred_element_type=jnp.float32)
    labels = jnp.arange(EXPERTS, dtype=jnp.int32)
    picked = (expert_ids[:, :, None] == labels[None, None, :]).astype(jnp.float32)
    chosen = lax.optimization_barrier(jnp.sum(picked * logits[:, None, :], axis=2))
    first_gate = jax.nn.sigmoid(chosen[:, 0] - chosen[:, 1])
    gate_pair = jnp.stack([first_gate, 1.0 - first_gate], axis=1)
    block_ids = expert_ids.reshape(N_DP, TOK_DEV * 2)
    ids_onehot = (block_ids[:, :, None] == labels[None, None, :]).astype(jnp.int32)
    earlier = jnp.cumsum(ids_onehot, axis=1) - ids_onehot
    slot_index = lax.optimization_barrier(jnp.sum(earlier * ids_onehot, axis=2))
    sources = lax.broadcasted_iota(jnp.int32, (N_DP, TOK_DEV * 2), 0)
    places = (sources * CAP + slot_index).reshape(-1).astype(jnp.int32)
    flat_ids = expert_ids.reshape(-1).astype(jnp.int32)

    def place_rows(token_rows):
        return jnp.zeros((EXPERTS, N_DP * CAP, D), jnp.bfloat16).at[flat_ids, places].set(token_rows)
    expert_rows = place_rows(jnp.repeat(normed_two, 2, axis=0))
    cot_f = out_cotangent.astype(jnp.float32)
    cot_rows = (gate_pair[:, :, None] * cot_f[:, None, :]).astype(jnp.bfloat16).reshape(TOKENS * 2, D)
    expert_drows = place_rows(cot_rows)

    def one_expert(member_set):
        rows_in, drows_in, weight_in, weight_out = member_set
        pre_act, active, owner_out = expert_forward(rows_in, weight_in, weight_out)
        grad_in, grad_out, owner_back = expert_backward(rows_in, pre_act, active, drows_in, weight_in, weight_out)
        return (owner_out.astype(jnp.bfloat16), owner_back.astype(jnp.bfloat16), grad_in, grad_out)
    results, row_grads, expert_in_grad, expert_out_grad = lax.map(one_expert, (expert_rows, expert_drows, expert_in, expert_out))
    result_rows = results[flat_ids, places].reshape(TOKENS, 2, D).astype(jnp.float32)
    mixture = lax.optimization_barrier(jnp.sum(gate_pair[:, :, None] * result_rows, axis=1))
    block_output = (residual + mixture).astype(jnp.bfloat16)
    gate_grads = lax.optimization_barrier(jnp.sum(cot_f[:, None, :] * result_rows, axis=2))
    dlogit = (gate_grads[:, 0] - gate_grads[:, 1]) * first_gate * (1.0 - first_gate)
    signed = jnp.stack([dlogit, -dlogit], axis=1)
    dlogits = lax.optimization_barrier(jnp.sum(picked * signed[:, :, None], axis=1)).astype(jnp.bfloat16)
    router_grad = jnp.dot(normed_two.T, dlogits, preferred_element_type=jnp.float32)
    back_rows = row_grads[flat_ids, places].reshape(TOKENS, 2, D).astype(jnp.float32)
    dnormed_two = lax.optimization_barrier(jnp.sum(back_rows, axis=1)) + jnp.dot(dlogits, router_weight.T, preferred_element_type=jnp.float32)
    ffn_gain_grad = lax.optimization_barrier(jnp.sum(dnormed_two * residual * scale_two, axis=0))
    dresidual = cot_f + norm_back(dnormed_two, residual, scale_two, gain_two)
    dres_low = dresidual.astype(jnp.bfloat16)
    output_grad = jnp.dot(dres_low.T, context_flat, preferred_element_type=jnp.float32)
    dcontext = jnp.dot(dres_low, output_weight, preferred_element_type=jnp.float32).astype(jnp.bfloat16)

    def backward_one(member_set):
        return attend_backward(member_set[0], member_set[1], member_set[2], bias_heads, causal, member_set[3], member_set[4], bucket_vec, NB)
    dqueries, dkeys, dvalues, dbias = lax.map(backward_one, (split_heads(queries), split_heads(key_rows), split_heads(value_rows), log_total, split_heads(dcontext)))
    bias_grad = lax.optimization_barrier(jnp.sum(dbias, axis=0))
    dq_flat = dqueries.reshape(TOKENS, HD_ALL)
    dk_flat = dkeys.reshape(TOKENS, HD_ALL)
    dv_flat = dvalues.reshape(TOKENS, HD_ALL)
    query_grad = jnp.dot(normed_one.T, dq_flat, preferred_element_type=jnp.float32)
    key_grad = jnp.dot(normed_one.T, dk_flat, preferred_element_type=jnp.float32)
    value_grad = jnp.dot(normed_one.T, dv_flat, preferred_element_type=jnp.float32)
    dnormed_one = jnp.dot(dq_flat, query_weight.T, preferred_element_type=jnp.float32)
    dnormed_one = dnormed_one + jnp.dot(dk_flat, key_weight.T, preferred_element_type=jnp.float32)
    dnormed_one = dnormed_one + jnp.dot(dv_flat, value_weight.T, preferred_element_type=jnp.float32)
    attn_gain_grad = lax.optimization_barrier(jnp.sum(dnormed_one * inputs_f * scale_one, axis=0))
    input_grad = dresidual + norm_back(dnormed_one, inputs_f, scale_one, gain_one)
    return (block_output, input_grad, attn_gain_grad, query_grad, key_grad, value_grad, output_grad, bias_grad, ffn_gain_grad, router_grad, expert_in_grad, expert_out_grad)
```

```python
import math

import jax
import jax.numpy as jnp
from jax import lax
from jax.experimental import pallas as pl
from jax.experimental.pallas import tpu as pltpu
from jax.sharding import PartitionSpec as P

HEAD_DIM = 64
NB = 32
SEQ_LEN = 512
LANES = 128


EPSILON = 1e-06
MASKED = -1e30


def bucket_vector_at(steps_ids, bucket_count):
    exact_count = bucket_count // 2
    distant = jnp.full(steps_ids.shape, exact_count, jnp.int32)
    for level_index in range(1, bucket_count - exact_count):
        border = int(math.ceil(exact_count * 8.0 ** (level_index / (bucket_count - exact_count))))
        distant = distant + (steps_ids >= border).astype(jnp.int32)
    return jnp.where(steps_ids < exact_count, steps_ids, distant)


def norm_back(dnormed, row_values, row_scale, gain_row):
    inner_mean = jnp.mean(gain_row * dnormed * row_values, axis=-1, keepdims=True)
    return row_scale * (gain_row * dnormed - row_values * row_scale * row_scale * inner_mean)


def rms_scale(matrix):
    return lax.rsqrt(jnp.mean(matrix * matrix, axis=-1, keepdims=True) + EPSILON)


def dot(left, right, dims=((1,), (0,))):
    return lax.dot_general(left, right, (dims, ((), ())), preferred_element_type=jnp.float32)


def forward_kernel(qkv_ref, wrapped_ref, context_ref, probs_ref):
    length = qkv_ref.shape[0]
    heads = probs_ref.shape[0]
    width = heads * HEAD_DIM
    factor = HEAD_DIM ** (-0.5)
    rows = lax.broadcasted_iota(jnp.int32, (length, length), 0)
    cols = lax.broadcasted_iota(jnp.int32, (length, length), 1)
    causal = rows >= cols
    for h in range(heads):
        lo, hi = h * HEAD_DIM, (h + 1) * HEAD_DIM
        queries = qkv_ref[:, lo:hi]
        keys = qkv_ref[:, width + lo : width + hi]
        values = qkv_ref[:, 2 * width + lo : 2 * width + hi]
        bias = jnp.broadcast_to(wrapped_ref[h : h + 1, :], (length, length))
        bias = pltpu.roll(bias, 0, 1, stride=1, stride_axis=0)
        scores = jnp.where(causal, dot(queries, keys, ((1,), (1,))) * factor + bias, MASKED)
        row_max = jnp.max(scores, axis=-1, keepdims=True)
        row_total = jnp.sum(jnp.exp(scores - row_max), axis=-1, keepdims=True)
        probs = jnp.exp(scores - (row_max + jnp.log(row_total))).astype(jnp.bfloat16)
        probs_ref[h] = probs
        context_ref[:, lo:hi] = dot(probs, values).astype(jnp.bfloat16)


def backward_kernel(qkv_ref, probs_ref, dcontext_ref, dqkv_ref, diagonal_ref):
    length = qkv_ref.shape[0]
    heads = probs_ref.shape[0]
    width = heads * HEAD_DIM
    factor = HEAD_DIM ** (-0.5)
    rows = lax.broadcasted_iota(jnp.int32, (length, length), 0)
    cols = lax.broadcasted_iota(jnp.int32, (length, length), 1)
    flip = (rows + cols == length - 1).astype(jnp.float32).astype(jnp.bfloat16)
    for h in range(heads):
        lo, hi = h * HEAD_DIM, (h + 1) * HEAD_DIM
        queries = qkv_ref[:, lo:hi]
        keys = qkv_ref[:, width + lo : width + hi]
        values = qkv_ref[:, 2 * width + lo : 2 * width + hi]
        dcontext = dcontext_ref[:, lo:hi]
        probs = probs_ref[h]
        weights = probs.astype(jnp.float32)
        dweights = dot(dcontext, values, ((1,), (1,)))
        agreement = jnp.sum(weights * dweights, axis=-1, keepdims=True)
        dscores = (weights * (dweights - agreement)).astype(jnp.bfloat16)
        dqkv_ref[:, lo:hi] = (factor * dot(dscores, keys)).astype(jnp.bfloat16)
        dqkv_ref[:, width + lo : width + hi] = (
            factor * dot(dscores, queries, ((0,), (0,)))
        ).astype(jnp.bfloat16)
        dqkv_ref[:, 2 * width + lo : 2 * width + hi] = dot(
            probs, dcontext, ((0,), (0,))
        ).astype(jnp.bfloat16)
        skewed = pltpu.roll(dot(flip, dscores), 0, 1, stride=1, stride_axis=0)
        diagonal_ref[h : h + 1, :] = jnp.sum(skewed, axis=0, keepdims=True)


def attend_forward(qkv, wrapped, seq_count, heads):
    width = heads * HEAD_DIM
    return pl.pallas_call(
        forward_kernel,
        grid=(seq_count,),
        out_shape=(
            jax.ShapeDtypeStruct((seq_count * SEQ_LEN, width), jnp.bfloat16),
            jax.ShapeDtypeStruct((seq_count, heads, SEQ_LEN, SEQ_LEN), jnp.bfloat16),
        ),
        in_specs=[
            pl.BlockSpec((SEQ_LEN, 3 * width), lambda s: (s, 0)),
            pl.BlockSpec((heads, SEQ_LEN), lambda s: (0, 0)),
        ],
        out_specs=(
            pl.BlockSpec((SEQ_LEN, width), lambda s: (s, 0)),
            pl.BlockSpec((None, heads, SEQ_LEN, SEQ_LEN), lambda s: (s, 0, 0, 0)),
        ),
        name="attend_forward",
    )(qkv, wrapped)


def attend_backward(qkv, probs, dcontext, seq_count, heads):
    width = heads * HEAD_DIM
    return pl.pallas_call(
        backward_kernel,
        grid=(seq_count,),
        out_shape=(
            jax.ShapeDtypeStruct((seq_count * SEQ_LEN, 3 * width), jnp.bfloat16),
            jax.ShapeDtypeStruct((seq_count, heads, SEQ_LEN), jnp.float32),
        ),
        in_specs=[
            pl.BlockSpec((SEQ_LEN, 3 * width), lambda s: (s, 0)),
            pl.BlockSpec((None, heads, SEQ_LEN, SEQ_LEN), lambda s: (s, 0, 0, 0)),
            pl.BlockSpec((SEQ_LEN, width), lambda s: (s, 0)),
        ],
        out_specs=(
            pl.BlockSpec((SEQ_LEN, 3 * width), lambda s: (s, 0)),
            pl.BlockSpec((None, heads, SEQ_LEN), lambda s: (s, 0, 0)),
        ),
        name="attend_backward",
    )(qkv, probs, dcontext)


def exchange(parcel):
    return lax.all_to_all(parcel, "dp", split_axis=0, concat_axis=0, tiled=True)


def on_device(
    block_input,
    attn_gain,
    query_weight,
    key_weight,
    value_weight,
    output_weight,
    bias_table,
    ffn_gain,
    router_weight,
    expert_in,
    expert_out,
    expert_ids,
    out_cotangent,
):
    tensor_size = lax.axis_size("tensor")
    group_size = lax.axis_size("dp")
    tensor_index = lax.axis_index("tensor")
    own_expert = lax.axis_index("dp")
    token_count, model_width = block_input.shape
    column_width = model_width // tensor_size
    column_start = tensor_index * column_width
    expert_count = group_size * expert_in.shape[0]
    capacity = tensor_size * max(1, 3 * token_count // (5 * expert_count))
    slot_rows = expert_count * capacity
    seq_count = token_count // SEQ_LEN
    head_local = bias_table.shape[0]
    head_width = head_local * HEAD_DIM
    block_rows = query_weight.shape[0]
    low = jnp.bfloat16

    def own_columns(matrix):
        return lax.dynamic_slice_in_dim(matrix, column_start, column_width, 1)

    packed = jnp.concatenate(
        [
            query_weight,
            key_weight,
            value_weight,
            output_weight,
            router_weight,
            attn_gain[:, None],
            ffn_gain[:, None],
        ],
        axis=1,
    )
    packed = lax.all_gather(packed, "dp", axis=0, tiled=True)
    qkv_full = packed[:, : 3 * head_width]
    output_full = packed[:, 3 * head_width : 4 * head_width]
    at = 4 * head_width
    router_full = packed[:, at : at + expert_count]
    gain_one = packed[:, at + expert_count].astype(jnp.float32)
    gain_two = packed[:, at + expert_count + 1].astype(jnp.float32)

    labels = jnp.arange(expert_count, dtype=jnp.int32)
    flat_ids = expert_ids.reshape(-1)
    ids_onehot = (flat_ids[:, None] == labels[None, :]).astype(jnp.int32)
    pair_rows = lax.broadcasted_iota(jnp.int32, (2 * token_count, 2 * token_count), 0)
    pair_cols = lax.broadcasted_iota(jnp.int32, (2 * token_count, 2 * token_count), 1)
    before = (pair_cols < pair_rows).astype(low)
    earlier = dot(before, ids_onehot.astype(low)).astype(jnp.int32)
    slot_index = jnp.sum(earlier * ids_onehot, axis=1)
    places = (flat_ids * capacity + slot_index).reshape(token_count, 2)
    place_rows = jnp.arange(slot_rows, dtype=jnp.int32)
    at_first = places[:, 0][None, :] == place_rows[:, None]
    at_second = places[:, 1][None, :] == place_rows[:, None]
    map_first = at_first.astype(low)
    map_second = at_second.astype(low)
    map_both = (at_first | at_second).astype(low)

    ids_low = jnp.broadcast_to(expert_ids.astype(low)[:, :, None], (token_count, 2, LANES))
    cot_source = jnp.concatenate(
        [
            jnp.concatenate([out_cotangent, ids_low[:, 1]], axis=1),
            jnp.concatenate([out_cotangent, ids_low[:, 0]], axis=1),
        ],
        axis=0,
    )
    cot_parcel = dot(jnp.concatenate([map_first, map_second], axis=1), cot_source).astype(low)
    cot_arrived = exchange(
        cot_parcel.reshape(expert_count, capacity, model_width + LANES)
    ).reshape(slot_rows, model_width + LANES)
    cot_rows = cot_arrived[:, :model_width].astype(jnp.float32)
    other_ids = cot_arrived[:, model_width].astype(jnp.int32)

    inputs_f = block_input.astype(jnp.float32)
    scale_one = rms_scale(inputs_f)
    normed_one = (inputs_f * scale_one * gain_one).astype(low)
    qkv = dot(normed_one, qkv_full).astype(low)
    bucket_vec = bucket_vector_at(jnp.arange(SEQ_LEN, dtype=jnp.int32), NB)
    bucket_labels = jnp.arange(NB, dtype=jnp.int32)
    wrap = (SEQ_LEN - jnp.arange(SEQ_LEN, dtype=jnp.int32)) % SEQ_LEN
    wrapped_onehot = bucket_vector_at(wrap, NB)[None, :] == bucket_labels[:, None]
    wrapped = jnp.sum(
        jnp.where(wrapped_onehot[None], bias_table[:, :, None], 0.0), axis=1
    )
    context, probs = attend_forward(qkv, wrapped, seq_count, head_local)
    attn_part = dot(context, output_full, ((1,), (1,))).astype(low)
    attn_out = lax.psum(attn_part, "tensor").astype(jnp.float32)
    residual = inputs_f + attn_out
    scale_two = rms_scale(residual)
    normed_two = (residual * scale_two * gain_two).astype(low)

    logits = dot(normed_two, router_full)
    picked = (expert_ids[:, :, None] == labels[None, None, :]).astype(jnp.float32)
    chosen = jnp.sum(picked * logits[:, None, :], axis=2)
    first_gate = jax.nn.sigmoid(chosen[:, 0] - chosen[:, 1])
    second_gate = 1.0 - first_gate

    weight_in = expert_in[0]
    weight_out = expert_out[0]
    parcel = dot(map_both, normed_two).astype(low)
    expert_rows = exchange(parcel.reshape(expert_count, capacity, model_width)).reshape(
        slot_rows, model_width
    )
    pre_act = dot(expert_rows, weight_in)
    active, pullback = jax.vjp(jax.nn.gelu, pre_act)
    active = active.astype(low)
    owner_out = dot(active, weight_out)
    owner_logits = dot(expert_rows, router_full)
    own_logit = jnp.sum(
        jnp.where(labels[None, :] == own_expert, owner_logits, 0.0), axis=1
    )
    other_logit = jnp.sum(
        jnp.where(labels[None, :] == other_ids[:, None], owner_logits, 0.0), axis=1
    )
    row_gate = jax.nn.sigmoid(own_logit - other_logit)
    expert_drows = (row_gate[:, None] * cot_rows).astype(low)
    dpre = pullback(dot(expert_drows, weight_out, ((1,), (1,))))[0].astype(low)
    owner_back = dot(dpre, weight_in, ((1,), (1,))).astype(low)
    gate_part = jnp.sum(cot_rows * owner_out, axis=1, keepdims=True).astype(low)
    back_parcel = jnp.concatenate(
        [owner_back, jnp.broadcast_to(gate_part, (slot_rows, LANES))], axis=1
    )
    back_rows = exchange(
        back_parcel.reshape(group_size, capacity, model_width + LANES)
    ).reshape(slot_rows, model_width + LANES)
    out_rows = exchange(
        owner_out.astype(low).reshape(group_size, capacity, model_width)
    ).reshape(slot_rows, model_width)
    out_grad = dot(active, expert_drows, ((0,), (0,)))
    in_grad = dot(expert_rows, dpre, ((0,), (0,)))

    dnormed_part = dot(map_both, back_rows[:, :model_width], ((0,), (0,)))
    gate_diff_part = dot(map_first - map_second, back_rows[:, model_width:], ((0,), (0,)))
    summed = lax.psum(
        jnp.concatenate([dnormed_part, gate_diff_part], axis=1).astype(low), "tensor"
    ).astype(jnp.float32)
    mixture_part = first_gate[:, None] * dot(map_first, out_rows, ((0,), (0,)))
    mixture_part = mixture_part + second_gate[:, None] * dot(
        map_second, out_rows, ((0,), (0,))
    )
    mixture = lax.psum_scatter(
        mixture_part.astype(low), "tensor", scatter_dimension=1, tiled=True
    ).astype(jnp.float32)
    block_output = (own_columns(residual) + mixture).astype(low)

    dlogit = summed[:, model_width] * first_gate * second_gate
    signed = jnp.stack([dlogit, -dlogit], axis=1)
    dlogits = jnp.sum(picked * signed[:, :, None], axis=1).astype(low)
    router_term = dot(normed_two, dlogits, ((0,), (0,)))
    dnormed_two = summed[:, :model_width] + dot(dlogits, router_full, ((1,), (1,)))
    ffn_term = jnp.sum(dnormed_two * residual * scale_two, axis=0)
    cot_f = out_cotangent.astype(jnp.float32)
    dresidual = cot_f + norm_back(dnormed_two, residual, scale_two, gain_two)
    dres_low = dresidual.astype(low)

    output_term = dot(dres_low, context, ((0,), (0,)))
    dcontext = dot(dres_low, output_full).astype(low)
    dqkv, diagonal = attend_backward(qkv, probs, dcontext, seq_count, head_local)
    reverse_onehot = (bucket_vec[::-1][:, None] == bucket_labels[None, :]).astype(jnp.float32)
    bias_term = jnp.dot(
        jnp.sum(diagonal, axis=0),
        reverse_onehot,
        precision=lax.Precision.HIGHEST,
        preferred_element_type=jnp.float32,
    )
    dnormed_one = lax.psum(
        dot(dqkv, qkv_full, ((1,), (1,))).astype(low), "tensor"
    ).astype(jnp.float32)
    qkv_term = dot(normed_one, dqkv, ((0,), (0,)))
    attn_term = jnp.sum(dnormed_one * inputs_f * scale_one, axis=0)
    first_back = norm_back(dnormed_one, inputs_f, scale_one, gain_one)
    input_grad = own_columns(dresidual + first_back)

    bias_count = bias_term.size
    bias_cols = -(-bias_count // block_rows)
    bias_block = jnp.pad(bias_term.reshape(-1), (0, bias_cols * block_rows - bias_count))
    bias_block = jnp.tile(bias_block.reshape(block_rows, bias_cols), (group_size, 1))
    terms = jnp.concatenate(
        [qkv_term, output_term, router_term, attn_term[:, None], ffn_term[:, None], bias_block],
        axis=1,
    ).astype(low)
    term_width = terms.shape[1]
    arrived = exchange(terms.reshape(group_size, block_rows, term_width))
    reduced = jnp.sum(arrived.astype(jnp.float32), axis=0)
    at = 4 * head_width
    grads = [reduced[:, k * head_width : (k + 1) * head_width] for k in range(4)]
    router_grad = reduced[:, at : at + expert_count]
    at = at + expert_count
    bias_grad = reduced[:, at + 2 :].reshape(-1)[:bias_count].reshape(bias_term.shape)
    return (
        block_output,
        input_grad,
        reduced[:, at],
        grads[0],
        grads[1],
        grads[2],
        grads[3],
        bias_grad,
        reduced[:, at + 1],
        router_grad,
        in_grad[None],
        out_grad[None],
    )


def solution(mesh):
    placed = (
        P("dp", None),
        P("dp"),
        P("dp", "tensor"),
        P("dp", "tensor"),
        P("dp", "tensor"),
        P("dp", "tensor"),
        P("tensor", None),
        P("dp"),
        P("dp", None),
        P("dp", None, "tensor"),
        P("dp", "tensor", None),
        P("dp", None),
        P("dp", None),
    )
    return jax.shard_map(
        on_device,
        mesh=mesh,
        in_specs=placed,
        out_specs=(
            P("dp", "tensor"),
            P("dp", "tensor"),
            P("dp"),
            P("dp", "tensor"),
            P("dp", "tensor"),
            P("dp", "tensor"),
            P("dp", "tensor"),
            P("tensor", None),
            P("dp"),
            P("dp", None),
            P("dp", None, "tensor"),
            P("dp", "tensor", None),
        ),
        check_vma=False,
    )
```

```python
import math

import jax
import jax.numpy as jnp
from jax import lax
from jax.experimental import pallas as pl
from jax.experimental.pallas import tpu as pltpu
from jax.sharding import PartitionSpec as P

HEAD_DIM = 64
NB = 32
SEQ_LEN = 512
LANES = 128


EPSILON = 1e-06
MASKED = -1e30


def bucket_vector_at(steps_ids, bucket_count):
    exact_count = bucket_count // 2
    distant = jnp.full(steps_ids.shape, exact_count, jnp.int32)
    for level_index in range(1, bucket_count - exact_count):
        border = int(math.ceil(exact_count * 8.0 ** (level_index / (bucket_count - exact_count))))
        distant = distant + (steps_ids >= border).astype(jnp.int32)
    return jnp.where(steps_ids < exact_count, steps_ids, distant)


def norm_back(dnormed, row_values, row_scale, gain_row):
    inner_mean = jnp.mean(gain_row * dnormed * row_values, axis=-1, keepdims=True)
    return row_scale * (gain_row * dnormed - row_values * row_scale * row_scale * inner_mean)


def rms_scale(matrix):
    return lax.rsqrt(jnp.mean(matrix * matrix, axis=-1, keepdims=True) + EPSILON)


def dot(left, right, dims=((1,), (0,))):
    return lax.dot_general(left, right, (dims, ((), ())), preferred_element_type=jnp.float32)


def forward_kernel(qkv_ref, wrapped_ref, context_ref, probs_ref):
    length = qkv_ref.shape[0]
    heads = probs_ref.shape[0]
    width = heads * HEAD_DIM
    factor = HEAD_DIM ** (-0.5)
    rows = lax.broadcasted_iota(jnp.int32, (length, length), 0)
    cols = lax.broadcasted_iota(jnp.int32, (length, length), 1)
    causal = rows >= cols
    for h in range(heads):
        lo, hi = h * HEAD_DIM, (h + 1) * HEAD_DIM
        queries = qkv_ref[:, lo:hi]
        keys = qkv_ref[:, width + lo : width + hi]
        values = qkv_ref[:, 2 * width + lo : 2 * width + hi]
        bias = jnp.broadcast_to(wrapped_ref[h : h + 1, :], (length, length))
        bias = pltpu.roll(bias, 0, 1, stride=1, stride_axis=0)
        scores = jnp.where(causal, dot(queries, keys, ((1,), (1,))) * factor + bias, MASKED)
        row_max = jnp.max(scores, axis=-1, keepdims=True)
        row_total = jnp.sum(jnp.exp(scores - row_max), axis=-1, keepdims=True)
        probs = jnp.exp(scores - (row_max + jnp.log(row_total))).astype(jnp.bfloat16)
        probs_ref[h] = probs
        context_ref[:, lo:hi] = dot(probs, values).astype(jnp.bfloat16)


def backward_kernel(qkv_ref, probs_ref, dcontext_ref, dqkv_ref, diagonal_ref):
    length = qkv_ref.shape[0]
    heads = probs_ref.shape[0]
    width = heads * HEAD_DIM
    factor = HEAD_DIM ** (-0.5)
    rows = lax.broadcasted_iota(jnp.int32, (length, length), 0)
    cols = lax.broadcasted_iota(jnp.int32, (length, length), 1)
    flip = (rows + cols == length - 1).astype(jnp.float32).astype(jnp.bfloat16)
    for h in range(heads):
        lo, hi = h * HEAD_DIM, (h + 1) * HEAD_DIM
        queries = qkv_ref[:, lo:hi]
        keys = qkv_ref[:, width + lo : width + hi]
        values = qkv_ref[:, 2 * width + lo : 2 * width + hi]
        dcontext = dcontext_ref[:, lo:hi]
        probs = probs_ref[h]
        weights = probs.astype(jnp.float32)
        dweights = dot(dcontext, values, ((1,), (1,)))
        agreement = jnp.sum(weights * dweights, axis=-1, keepdims=True)
        dscores = (weights * (dweights - agreement)).astype(jnp.bfloat16)
        dqkv_ref[:, lo:hi] = (factor * dot(dscores, keys)).astype(jnp.bfloat16)
        dqkv_ref[:, width + lo : width + hi] = (
            factor * dot(dscores, queries, ((0,), (0,)))
        ).astype(jnp.bfloat16)
        dqkv_ref[:, 2 * width + lo : 2 * width + hi] = dot(
            probs, dcontext, ((0,), (0,))
        ).astype(jnp.bfloat16)
        skewed = pltpu.roll(dot(flip, dscores), 0, 1, stride=1, stride_axis=0)
        diagonal_ref[h : h + 1, :] = jnp.sum(skewed, axis=0, keepdims=True)


def attend_forward(qkv, wrapped, seq_count, heads):
    width = heads * HEAD_DIM
    return pl.pallas_call(
        forward_kernel,
        grid=(seq_count,),
        out_shape=(
            jax.ShapeDtypeStruct((seq_count * SEQ_LEN, width), jnp.bfloat16),
            jax.ShapeDtypeStruct((seq_count, heads, SEQ_LEN, SEQ_LEN), jnp.bfloat16),
        ),
        in_specs=[
            pl.BlockSpec((SEQ_LEN, 3 * width), lambda s: (s, 0)),
            pl.BlockSpec((heads, SEQ_LEN), lambda s: (0, 0)),
        ],
        out_specs=(
            pl.BlockSpec((SEQ_LEN, width), lambda s: (s, 0)),
            pl.BlockSpec((None, heads, SEQ_LEN, SEQ_LEN), lambda s: (s, 0, 0, 0)),
        ),
        name="attend_forward",
    )(qkv, wrapped)


def attend_backward(qkv, probs, dcontext, seq_count, heads):
    width = heads * HEAD_DIM
    return pl.pallas_call(
        backward_kernel,
        grid=(seq_count,),
        out_shape=(
            jax.ShapeDtypeStruct((seq_count * SEQ_LEN, 3 * width), jnp.bfloat16),
            jax.ShapeDtypeStruct((seq_count, heads, SEQ_LEN), jnp.float32),
        ),
        in_specs=[
            pl.BlockSpec((SEQ_LEN, 3 * width), lambda s: (s, 0)),
            pl.BlockSpec((None, heads, SEQ_LEN, SEQ_LEN), lambda s: (s, 0, 0, 0)),
            pl.BlockSpec((SEQ_LEN, width), lambda s: (s, 0)),
        ],
        out_specs=(
            pl.BlockSpec((SEQ_LEN, 3 * width), lambda s: (s, 0)),
            pl.BlockSpec((None, heads, SEQ_LEN), lambda s: (s, 0, 0)),
        ),
        name="attend_backward",
    )(qkv, probs, dcontext)


def exchange(parcel):
    return lax.all_to_all(parcel, "dp", split_axis=0, concat_axis=0, tiled=True)


def on_device(
    block_input,
    attn_gain,
    query_weight,
    key_weight,
    value_weight,
    output_weight,
    bias_table,
    ffn_gain,
    router_weight,
    expert_in,
    expert_out,
    expert_ids,
    out_cotangent,
):
    tensor_size = lax.axis_size("tensor")
    group_size = lax.axis_size("dp")
    tensor_index = lax.axis_index("tensor")
    own_expert = lax.axis_index("dp")
    token_count, model_width = block_input.shape
    column_width = model_width // tensor_size
    column_start = tensor_index * column_width
    expert_count = group_size * expert_in.shape[0]
    capacity = tensor_size * max(1, 3 * token_count // (5 * expert_count))
    slot_rows = expert_count * capacity
    seq_count = token_count // SEQ_LEN
    head_local = bias_table.shape[0]
    head_width = head_local * HEAD_DIM
    block_rows = query_weight.shape[0]
    low = jnp.bfloat16

    def own_columns(matrix):
        return lax.dynamic_slice_in_dim(matrix, column_start, column_width, 1)

    packed = jnp.concatenate(
        [
            query_weight,
            key_weight,
            value_weight,
            output_weight,
            router_weight,
            attn_gain[:, None],
            ffn_gain[:, None],
        ],
        axis=1,
    )
    packed = lax.all_gather(packed, "dp", axis=0, tiled=True)

    labels = jnp.arange(expert_count, dtype=jnp.int32)
    flat_ids = expert_ids.reshape(-1)
    ids_onehot = (flat_ids[:, None] == labels[None, :]).astype(jnp.int32)
    pair_rows = lax.broadcasted_iota(jnp.int32, (2 * token_count, 2 * token_count), 0)
    pair_cols = lax.broadcasted_iota(jnp.int32, (2 * token_count, 2 * token_count), 1)
    before = (pair_cols < pair_rows).astype(low)
    earlier = dot(before, ids_onehot.astype(low)).astype(jnp.int32)
    slot_index = jnp.sum(earlier * ids_onehot, axis=1)
    places = (flat_ids * capacity + slot_index).reshape(token_count, 2)
    place_rows = jnp.arange(slot_rows, dtype=jnp.int32)
    at_first = places[:, 0][None, :] == place_rows[:, None]
    at_second = places[:, 1][None, :] == place_rows[:, None]
    map_first = at_first.astype(low)
    map_second = at_second.astype(low)
    map_both = (at_first | at_second).astype(low)

    ids_low = jnp.broadcast_to(expert_ids.astype(low)[:, :, None], (token_count, 2, LANES))
    cot_source = jnp.concatenate(
        [
            jnp.concatenate([out_cotangent, ids_low[:, 1]], axis=1),
            jnp.concatenate([out_cotangent, ids_low[:, 0]], axis=1),
        ],
        axis=0,
    )
    cot_parcel = dot(jnp.concatenate([map_first, map_second], axis=1), cot_source).astype(low)
    packed, cot_parcel = lax.optimization_barrier((packed, cot_parcel))
    cot_arrived = exchange(
        cot_parcel.reshape(expert_count, capacity, model_width + LANES)
    ).reshape(slot_rows, model_width + LANES)
    cot_rows = cot_arrived[:, :model_width].astype(jnp.float32)
    other_ids = cot_arrived[:, model_width].astype(jnp.int32)

    qkv_full = packed[:, : 3 * head_width]
    output_full = packed[:, 3 * head_width : 4 * head_width]
    at = 4 * head_width
    router_full = packed[:, at : at + expert_count]
    gain_one = packed[:, at + expert_count].astype(jnp.float32)
    gain_two = packed[:, at + expert_count + 1].astype(jnp.float32)
    inputs_f = block_input.astype(jnp.float32)
    scale_one = rms_scale(inputs_f)
    normed_one = (inputs_f * scale_one * gain_one).astype(low)
    qkv = dot(normed_one, qkv_full).astype(low)
    bucket_vec = bucket_vector_at(jnp.arange(SEQ_LEN, dtype=jnp.int32), NB)
    bucket_labels = jnp.arange(NB, dtype=jnp.int32)
    wrap = (SEQ_LEN - jnp.arange(SEQ_LEN, dtype=jnp.int32)) % SEQ_LEN
    wrapped_onehot = bucket_vector_at(wrap, NB)[None, :] == bucket_labels[:, None]
    wrapped = jnp.sum(
        jnp.where(wrapped_onehot[None], bias_table[:, :, None], 0.0), axis=1
    )
    context, probs = attend_forward(qkv, wrapped, seq_count, head_local)
    attn_part = dot(context, output_full, ((1,), (1,))).astype(low)
    attn_out = lax.psum(attn_part, "tensor").astype(jnp.float32)
    residual = inputs_f + attn_out
    scale_two = rms_scale(residual)
    normed_two = (residual * scale_two * gain_two).astype(low)

    logits = dot(normed_two, router_full)
    picked = (expert_ids[:, :, None] == labels[None, None, :]).astype(jnp.float32)
    chosen = jnp.sum(picked * logits[:, None, :], axis=2)
    first_gate = jax.nn.sigmoid(chosen[:, 0] - chosen[:, 1])
    second_gate = 1.0 - first_gate

    weight_in = expert_in[0]
    weight_out = expert_out[0]
    parcel = dot(map_both, normed_two).astype(low)
    expert_rows = exchange(parcel.reshape(expert_count, capacity, model_width)).reshape(
        slot_rows, model_width
    )
    pre_act = dot(expert_rows, weight_in)
    active, pullback = jax.vjp(jax.nn.gelu, pre_act)
    active = active.astype(low)
    owner_out = dot(active, weight_out)
    owner_logits = dot(expert_rows, router_full)
    own_logit = jnp.sum(
        jnp.where(labels[None, :] == own_expert, owner_logits, 0.0), axis=1
    )
    other_logit = jnp.sum(
        jnp.where(labels[None, :] == other_ids[:, None], owner_logits, 0.0), axis=1
    )
    row_gate = jax.nn.sigmoid(own_logit - other_logit)
    expert_drows = (row_gate[:, None] * cot_rows).astype(low)
    dpre = pullback(dot(expert_drows, weight_out, ((1,), (1,))))[0].astype(low)
    owner_back = dot(dpre, weight_in, ((1,), (1,))).astype(low)
    gate_part = jnp.sum(cot_rows * owner_out, axis=1, keepdims=True).astype(low)
    back_parcel = jnp.concatenate(
        [owner_back, jnp.broadcast_to(gate_part, (slot_rows, LANES))], axis=1
    )
    back_rows = exchange(
        back_parcel.reshape(group_size, capacity, model_width + LANES)
    ).reshape(slot_rows, model_width + LANES)
    out_rows = exchange(
        owner_out.astype(low).reshape(group_size, capacity, model_width)
    ).reshape(slot_rows, model_width)
    out_grad = dot(active, expert_drows, ((0,), (0,)))
    in_grad = dot(expert_rows, dpre, ((0,), (0,)))

    dnormed_part = dot(map_both, back_rows[:, :model_width], ((0,), (0,)))
    gate_diff_part = dot(map_first - map_second, back_rows[:, model_width:], ((0,), (0,)))
    gate_rows = -(-token_count // model_width)
    gate_line = jnp.pad(gate_diff_part[:, 0], (0, gate_rows * model_width - token_count))
    summed = lax.psum(
        jnp.concatenate(
            [dnormed_part, gate_line.reshape(gate_rows, model_width)], axis=0
        ).astype(low),
        "tensor",
    ).astype(jnp.float32)
    gate_diff = summed[token_count:].reshape(-1)[:token_count]
    mixture_part = first_gate[:, None] * dot(map_first, out_rows, ((0,), (0,)))
    mixture_part = mixture_part + second_gate[:, None] * dot(
        map_second, out_rows, ((0,), (0,))
    )
    mixture_parts = mixture_part.astype(low).reshape(token_count, tensor_size, column_width)
    mixture_parts = jnp.swapaxes(mixture_parts, 0, 1)

    dlogit = gate_diff * first_gate * second_gate
    signed = jnp.stack([dlogit, -dlogit], axis=1)
    dlogits = jnp.sum(picked * signed[:, :, None], axis=1).astype(low)
    router_term = dot(normed_two, dlogits, ((0,), (0,)))
    dnormed_two = summed[:token_count] + dot(dlogits, router_full, ((1,), (1,)))
    ffn_term = jnp.sum(dnormed_two * residual * scale_two, axis=0)
    cot_f = out_cotangent.astype(jnp.float32)
    dresidual = cot_f + norm_back(dnormed_two, residual, scale_two, gain_two)
    dres_low = dresidual.astype(low)
    mixture_parts, dres_low = lax.optimization_barrier((mixture_parts, dres_low))
    mixture_parts = lax.all_to_all(
        mixture_parts, "tensor", split_axis=0, concat_axis=0, tiled=True
    )

    output_term = dot(dres_low, context, ((0,), (0,)))
    dcontext = dot(dres_low, output_full).astype(low)
    dqkv, diagonal = attend_backward(qkv, probs, dcontext, seq_count, head_local)
    reverse_onehot = (bucket_vec[::-1][:, None] == bucket_labels[None, :]).astype(jnp.float32)
    bias_term = jnp.dot(
        jnp.sum(diagonal, axis=0),
        reverse_onehot,
        precision=lax.Precision.HIGHEST,
        preferred_element_type=jnp.float32,
    )
    dnormed_part = dot(dqkv, qkv_full, ((1,), (1,))).astype(low)
    dnormed_part, mixture_parts = lax.optimization_barrier((dnormed_part, mixture_parts))
    dnormed_one = lax.psum(dnormed_part, "tensor").astype(jnp.float32)
    qkv_term = dot(normed_one, dqkv, ((0,), (0,)))
    bias_count = bias_term.size
    bias_cols = -(-bias_count // block_rows)
    bias_block = jnp.pad(bias_term.reshape(-1), (0, bias_cols * block_rows - bias_count))
    bias_block = jnp.tile(bias_block.reshape(block_rows, bias_cols), (group_size, 1))
    terms = jnp.concatenate(
        [qkv_term, output_term, router_term, ffn_term[:, None], bias_block],
        axis=1,
    ).astype(low)
    term_width = terms.shape[1]
    arrived = exchange(terms.reshape(group_size, block_rows, term_width))
    arrived, dnormed_one = lax.optimization_barrier((arrived, dnormed_one))
    mixture = jnp.sum(mixture_parts.astype(jnp.float32), axis=0)
    block_output = (own_columns(residual) + mixture).astype(low)
    reduced = jnp.sum(arrived.astype(jnp.float32), axis=0)
    at = 4 * head_width
    grads = [reduced[:, k * head_width : (k + 1) * head_width] for k in range(4)]
    router_grad = reduced[:, at : at + expert_count]
    at = at + expert_count
    bias_grad = reduced[:, at + 1 :].reshape(-1)[:bias_count].reshape(bias_term.shape)
    attn_term = jnp.sum(dnormed_one * inputs_f * scale_one, axis=0)
    attn_gain_grad = jnp.sum(exchange(attn_term.reshape(group_size, block_rows)), axis=0)
    first_back = norm_back(dnormed_one, inputs_f, scale_one, gain_one)
    input_grad = own_columns(dresidual + first_back)
    return (
        block_output,
        input_grad,
        attn_gain_grad,
        grads[0],
        grads[1],
        grads[2],
        grads[3],
        bias_grad,
        reduced[:, at],
        router_grad,
        in_grad[None],
        out_grad[None],
    )


def solution(mesh):
    placed = (
        P("dp", None),
        P("dp"),
        P("dp", "tensor"),
        P("dp", "tensor"),
        P("dp", "tensor"),
        P("dp", "tensor"),
        P("tensor", None),
        P("dp"),
        P("dp", None),
        P("dp", None, "tensor"),
        P("dp", "tensor", None),
        P("dp", None),
        P("dp", None),
    )
    return jax.shard_map(
        on_device,
        mesh=mesh,
        in_specs=placed,
        out_specs=(
            P("dp", "tensor"),
            P("dp", "tensor"),
            P("dp"),
            P("dp", "tensor"),
            P("dp", "tensor"),
            P("dp", "tensor"),
            P("dp", "tensor"),
            P("tensor", None),
            P("dp"),
            P("dp", None),
            P("dp", None, "tensor"),
            P("dp", "tensor", None),
        ),
        check_vma=False,
    )
```
